32 devices in a mesh: brow: 4 (over z), bcol: 8 (over y, x, core).
Axes of the slice: x: 2, y: 2, z: 4, core: 2. Of those that a mesh axis runs over, the one named last changes fastest.
Arguments:
- anc_tiles: int32 [1, 12], replicated, may hold values from 0 to 31, as said below
- ancestor_inverse: float32 [16384, 16384], P('brow', 'bcol'), as said below
- factor_pieces: float32 [16384, 1536], P('bcol', 'brow'), may hold values from -6 to 6
Outputs:
- inverse_rows: float32 [1536, 16384], P('bcol', 'brow')
The draws below stay inside these ranges and needn't reach their ends.
Inputs may be any that keep to these rules, and one draw needn't show every extreme that they name: `anc_tiles`: each row lists 12 different tiles; tile 32 - 1 is listed in every row, tile 0 in row 0. ancestor_inverse is symmetric.
All inputs are finite; a program needn't handle non-finite values.
Results may differ from the reference program's by a relative error of at most 0.00007.
Values sent between devices are 32-bit elements; how exact they have to be, the bound alone decides.
A program may use at most 128 MiB of HBM per device.

```python
import jax
import jax.numpy as jnp
from jax import lax

TS = 512
W = 1536
A = 32
K = 1
M = 12
NANC = 16384
NCOL = 1536


def draw_anc_tiles(key, part):
    base = jax.random.randint(key, (K, A), 0, 4096)
    tile_ids = jnp.arange(A, dtype=jnp.int32)
    score = base + tile_ids[None, :] * 256
    row_ids = jnp.arange(K, dtype=jnp.int32)
    forced = (tile_ids[None, :] == A - 1) | (tile_ids[None, :] == 0) & (row_ids[:, None] == 0)
    score = jnp.where(forced, 1 << 22, score)
    score = score * A + tile_ids[None, :]
    values, chosen = lax.top_k(score, M)
    return chosen.astype(jnp.int32)


def draw_ancestor_inverse(key, part):
    noise = jax.random.normal(key, (NANC, NANC), jnp.float32)
    scale = 0.7071068 / (M * TS) ** 0.5
    index_row = jnp.arange(NANC)[:, None]
    index_col = jnp.arange(NANC)[None, :]
    diagonal = jnp.where(index_row == index_col, 1.0, 0.0).astype(jnp.float32)
    return ((noise + noise.T) * scale + diagonal).astype(jnp.float32)


def shard_levels(own_key, shape, shards, low, top_value):
    factor_of, own = 1.0, jax.random.fold_in(own_key, 6)
    for dim, parts in shards:
        draws = jnp.exp(jax.random.uniform(jax.random.fold_in(own, dim), (parts,), jnp.float32, low / len(shards), top_value / len(shards)))
        factor_of = factor_of * jnp.repeat(draws, shape[dim] // parts).reshape([-1 if axis == dim else 1 for axis in range(len(shape))])
    return factor_of


def bell_draw(stream_key, extent, scale, bound, cuts=(), held_as=jnp.bfloat16):
    result = jax.random.normal(stream_key, extent, jnp.float32) * scale
    if len(cuts) > 0:
        result = shard_levels(stream_key, extent, cuts, -0.22, 0.18) * result
    return jnp.clip(result, min=-bound, max=bound).astype(held_as)


def setup_inputs(seed: int = 0) -> dict:
    key_list = jax.random.split(jax.random.key(seed), 4)
    anc_tiles = draw_anc_tiles(jax.random.fold_in(key_list[3], 71), 0)
    ancestor_inverse = draw_ancestor_inverse(jax.random.fold_in(key_list[3], 71), 0)
    factor_pieces = bell_draw(key_list[2], (NANC, NCOL), 1.0, 6.0, ((0, 8), (1, 4)), jnp.float32)
    return {"anc_tiles": anc_tiles, "ancestor_inverse": ancestor_inverse, "factor_pieces": factor_pieces}


def reference(anc_tiles, ancestor_inverse, factor_pieces):
    tile_ids = jnp.arange(A, dtype=jnp.int32)
    listed = jnp.sum((anc_tiles[:, :, None] == tile_ids[None, None, :]).astype(jnp.int32), axis=1)
    listed_float = (listed > 0).astype(jnp.float32)
    row_mask = jnp.repeat(jnp.repeat(listed_float.T, TS, axis=0), W, axis=1)
    masked = factor_pieces * row_mask
    product = jnp.dot(ancestor_inverse, masked, precision=lax.Precision.HIGHEST, preferred_element_type=jnp.float32)
    return (-(product * row_mask)).T
```

```python
import jax
import jax.numpy as jnp
from jax import lax
from jax.sharding import PartitionSpec as P

TS = 512
W = 1536
A = 32
K = 1
CHUNKS = 4


def split(x):
    high = lax.reduce_precision(x, exponent_bits=8, mantissa_bits=7)
    return high.astype(jnp.bfloat16), (x - high).astype(jnp.bfloat16)


def product(x, y, **kwargs):
    return lax.dot_general(
        x, y, (((1,), (1,)), ((), ())), preferred_element_type=jnp.float32, **kwargs
    )


def local(anc_tiles, ancestor_inverse, factor_pieces):
    col_index = lax.axis_index("bcol")
    row_index = lax.axis_index("brow")
    n_col = lax.axis_size("bcol")
    n_row = lax.axis_size("brow")
    block_rows, block_cols = ancestor_inverse.shape
    tiles_col, tiles_row = block_cols // TS, block_rows // TS
    total_cols = factor_pieces.shape[1] * n_row
    tile_ids = jnp.arange(A, dtype=jnp.int32)
    listed = jnp.any(anc_tiles[:, :, None] == tile_ids[None, None, :], axis=1)

    col_super = (row_index * factor_pieces.shape[1] + jnp.arange(factor_pieces.shape[1])) // W
    listed_col = lax.dynamic_slice_in_dim(listed, col_index * tiles_col, tiles_col, 1)
    col_mask = jnp.repeat(listed_col[col_super], TS, axis=1)
    factor = jnp.where(col_mask, factor_pieces.T, 0.0)
    width = total_cols // n_col // CHUNKS
    factor = factor.reshape(-1, CHUNKS, width, block_cols)
    gathered = [
        lax.all_gather(factor[:, q], "brow", axis=0, tiled=True).reshape(-1, block_cols)
        for q in range(CHUNKS)
    ]

    sums = []
    for q in range(CHUNKS):
        part = product(gathered[q], ancestor_inverse, precision=lax.Precision.HIGH)
        sums.append(lax.psum_scatter(part, "bcol", scatter_dimension=0, tiled=True))
    summed = jnp.concatenate(sums, axis=0)

    out_rows = summed.shape[0]
    row_super = (col_index * out_rows + jnp.arange(out_rows)) // W
    listed_row = lax.dynamic_slice_in_dim(listed, row_index * tiles_row, tiles_row, 1)
    out_mask = jnp.repeat(listed_row[row_super], TS, axis=1)
    return jnp.where(out_mask, -summed, 0.0)


def solution(mesh):
    in_specs = (P(), P("brow", "bcol"), P("bcol", "brow"))
    out_specs = P("bcol", "brow")
    return jax.shard_map(local, mesh=mesh, in_specs=in_specs, out_specs=out_specs, check_vma=False)
```

```python
import jax
import jax.numpy as jnp
from jax import lax
from jax.sharding import PartitionSpec as P

TS = 512
W = 1536
A = 32
K = 1
CHUNKS = 3


def split(x):
    high = lax.reduce_precision(x, exponent_bits=8, mantissa_bits=7)
    return high.astype(jnp.bfloat16), (x - high).astype(jnp.bfloat16)


def product(x, y, **kwargs):
    return lax.dot_general(
        x, y, (((1,), (1,)), ((), ())), preferred_element_type=jnp.float32, **kwargs
    )


def line_gather(own, following, before, row_index, n_row):
    from_below, from_above = [], []
    below = above = own
    upward = [(r, r + 1) for r in range(n_row - 1)]
    downward = [(r + 1, r) for r in range(n_row - 1)]
    for step in range(n_row - 1):
        if step == n_row - 2 and following is not None:
            below, above, following = lax.optimization_barrier((below, above, following))
        if step == 1 and before is not None:
            below, above, before = lax.optimization_barrier((below, above, before))
        below = lax.ppermute(below, "brow", upward)
        above = lax.ppermute(above, "brow", downward)
        from_below.insert(0, below)
        from_above.append(above)
    window = jnp.stack(from_below + [own] + from_above)
    window = lax.dynamic_slice_in_dim(window, n_row - 1 - row_index, n_row, 0)
    return window.reshape(-1, own.shape[-1]), following, before


def local(anc_tiles, ancestor_inverse, factor_pieces):
    col_index = lax.axis_index("bcol")
    row_index = lax.axis_index("brow")
    n_col = lax.axis_size("bcol")
    n_row = lax.axis_size("brow")
    block_rows, block_cols = ancestor_inverse.shape
    tiles_col, tiles_row = block_cols // TS, block_rows // TS
    total_cols = factor_pieces.shape[1] * n_row
    tile_ids = jnp.arange(A, dtype=jnp.int32)
    listed = jnp.any(anc_tiles[:, :, None] == tile_ids[None, None, :], axis=1)

    col_super = (row_index * factor_pieces.shape[1] + jnp.arange(factor_pieces.shape[1])) // W
    listed_col = lax.dynamic_slice_in_dim(listed, col_index * tiles_col, tiles_col, 1)
    col_mask = jnp.repeat(listed_col[col_super], TS, axis=1)
    factor = jnp.where(col_mask, factor_pieces.T, 0.0)
    width = total_cols // n_col // CHUNKS
    factor = factor.reshape(-1, CHUNKS, width, block_cols)
    own = [factor[:, q] for q in range(CHUNKS)]
    parts = []
    for q in range(CHUNKS):
        following = own[q + 1] if q + 1 < CHUNKS else None
        before = parts[q - 1] if q > 0 else None
        whole, following, before = line_gather(own[q], following, before, row_index, n_row)
        if q > 0:
            parts[q - 1] = before
        if q + 1 < CHUNKS:
            own[q + 1] = following
        parts.append(product(whole, ancestor_inverse, precision=lax.Precision.HIGH))
    sums = [lax.psum_scatter(part, "bcol", scatter_dimension=0, tiled=True) for part in parts]
    summed = jnp.concatenate(sums, axis=0)

    out_rows = summed.shape[0]
    row_super = (col_index * out_rows + jnp.arange(out_rows)) // W
    listed_row = lax.dynamic_slice_in_dim(listed, row_index * tiles_row, tiles_row, 1)
    out_mask = jnp.repeat(listed_row[row_super], TS, axis=1)
    return jnp.where(out_mask, -summed, 0.0)


def solution(mesh):
    in_specs = (P(), P("brow", "bcol"), P("bcol", "brow"))
    out_specs = P("bcol", "brow")
    return jax.shard_map(local, mesh=mesh, in_specs=in_specs, out_specs=out_specs, check_vma=False)
```
